256 devices in a mesh: row: 16 (over y, x), col: 16 (over z, core).
Axes of the slice: x: 4, y: 4, z: 8, core: 2. Of those that a mesh axis runs over, the one named last changes fastest.
Arguments:
- matrix: float32 [20480, 8, 2048], P('row', None, 'col'), may hold values from -36 to 36, as said below
Outputs:
- factors: float32 [20480, 8, 2048], P('row', None, 'col')
- upper: float32 [256, 8, 2048], P(None, None, 'col')
The draws below stay inside these ranges and needn't reach their ends.
Inputs may be any that keep to these rules, and one draw needn't show every extreme that they name: A dense real matrix of full column rank.
All inputs are finite; a program needn't handle non-finite values.
Results may differ from the reference program's by a relative error of at most 0.0003.
Values sent between devices are 32-bit elements; how exact they have to be, the bound alone decides.
No kernel may reach another device: no remote copies, remote signals or barrier semaphores. Data moves between devices by JAX's collectives and lax.ppermute only.
A program may use at most 64 MiB of HBM per device.

```python
import math
import jax
import jax.numpy as jnp
from jax import lax

PANEL = 128
BLOCKS_DEV = 8
SPAN = 2048
ROWS = 20480


def draw_matrix(key, part):
    keys = jax.random.split(jax.random.fold_in(key, 11), 3)
    shape = (ROWS, BLOCKS_DEV, SPAN)
    row_scale = jnp.exp(jax.random.uniform(keys[1], (ROWS, 1, 1), jnp.float32, math.log(0.3), math.log(3.0)))
    col_scale = jnp.exp(jax.random.uniform(keys[2], (1, BLOCKS_DEV, SPAN), jnp.float32, math.log(0.3), math.log(3.0)))
    noise = jax.random.truncated_normal(keys[0], -4.0, 4.0, shape, jnp.float32)
    return (noise * row_scale * col_scale).astype(jnp.float32)


def setup_inputs(seed: int = 0) -> dict:
    streams_of = jax.random.split(jax.random.key(seed), 2)
    matrix = draw_matrix(jax.random.fold_in(streams_of[1], 71), 0)
    return {"matrix": matrix}


def upper_factor(gram):
    size = gram.shape[0]
    places = jnp.arange(size)

    def turn(j, carry):
        rest, lower = carry
        unit = (places == j).astype(gram.dtype)
        column = lax.optimization_barrier(jnp.sum(rest * unit[None, :], axis=1))
        pivot = jnp.sqrt(jnp.sum(column * unit))
        column = jnp.where(places >= j, column / pivot, jnp.zeros_like(column))
        rest = rest - column[:, None] * column[None, :]
        lower = lower + column[:, None] * unit[None, :]
        return (rest, lower)
    rest, lower = lax.fori_loop(0, size, turn, (gram, jnp.zeros_like(gram)))
    return lower.T

def upper_inverse(factor):
    size = factor.shape[0]
    places = jnp.arange(size)

    def turn(step, inverse):
        j = size - 1 - step
        unit = (places == j).astype(factor.dtype)
        row_vals = lax.optimization_barrier(jnp.sum(factor * unit[:, None], axis=0))
        pivot = jnp.sum(row_vals * unit)
        new_row = (unit - lax.optimization_barrier(jnp.sum(row_vals[:, None] * inverse, axis=0))) / pivot
        return inverse + unit[:, None] * new_row[None, :]
    return lax.fori_loop(0, size, turn, jnp.zeros_like(factor))

def orthonormal(panel):
    gram = jnp.dot(panel.T, panel, precision=lax.Precision.HIGHEST, preferred_element_type=jnp.float32)
    factor = upper_factor(gram)
    return jnp.dot(panel, upper_inverse(factor), precision=lax.Precision.HIGHEST, preferred_element_type=jnp.float32)

def project(basis, work):
    return jnp.einsum('rp,rbc->pbc', basis, work, precision=lax.Precision.HIGHEST, preferred_element_type=jnp.float32)

def remove(work, basis, coeffs):
    return work - jnp.einsum('rp,pbc->rbc', basis, coeffs, precision=lax.Precision.HIGHEST, preferred_element_type=jnp.float32)

def reference(matrix):
    scale = math.sqrt(ROWS)
    first = orthonormal(matrix[:, 0, 0:PANEL])
    coef_one = project(first, matrix)
    middle = remove(matrix, first, coef_one)
    second = orthonormal(middle[:, 0, PANEL:2 * PANEL])
    coef_two = project(second, middle)
    final = remove(middle, second, coef_two)
    factors = final.at[:, 0, 0:PANEL].set(first * scale)
    factors = factors.at[:, 0, PANEL:2 * PANEL].set(second * scale)
    upper = jnp.concatenate([coef_one, coef_two], axis=0) / scale
    return (factors, upper)
```

```python
import functools
import math

import jax
import jax.numpy as jnp
from jax import lax
from jax.experimental import pallas as pl
from jax.experimental.pallas import tpu as pltpu
from jax.sharding import PartitionSpec as P

F32 = jnp.float32
BF16 = jnp.bfloat16
HIGHEST = lax.Precision.HIGHEST
LANES = 128
SUB = 8


def split(x):
    high = x.astype(BF16)
    low = (x - high.astype(F32)).astype(BF16)
    return high, low


def dot3(a, b, dims=((1,), (0,))):
    mul = functools.partial(lax.dot_general, dimension_numbers=(dims, ((), ())), preferred_element_type=F32)
    return mul(a[0], b[0]) + (mul(a[0], b[1]) + mul(a[1], b[0]))


def dot6(a, b, dims=((1,), (0,))):
    return lax.dot_general(a, b, (dims, ((), ())), precision=HIGHEST, preferred_element_type=F32)


def gram_kernel(second_core, mine_ref, other_ref, m_ref, out_ref):
    rows = mine_ref.shape[0]
    blocks = m_ref.shape[0] // rows
    swapped = second_core[0] == 1
    mine, other = mine_ref[...], other_ref[...]
    panels = jnp.concatenate(
        [jnp.where(swapped, other, mine), jnp.where(swapped, mine, other)], axis=1
    )
    turned = panels.T
    left = split(turned)
    wide = blocks * LANES
    for k in range(0, blocks, 2):
        pair = jnp.concatenate(
            [m_ref[pl.ds(k, rows, stride=blocks), :], m_ref[pl.ds(k + 1, rows, stride=blocks), :]], axis=1
        )
        out_ref[:, k * LANES : (k + 2) * LANES] = dot3(left, split(pair))
    out_ref[:, wide : wide + 2 * LANES] = dot6(turned, panels)


def lower_inverse(tiles):
    count = len(tiles)
    tiles = list(tiles)
    lane = lax.broadcasted_iota(jnp.int32, (SUB, LANES), 1)
    row = lax.broadcasted_iota(jnp.int32, (SUB, LANES), 0)
    whole = lambda x: jnp.broadcast_to(x, (SUB, LANES))
    done = []
    for t in range(count):
        base = SUB * t
        here = tiles[t]
        inside = (lane >= base) & (lane < base + SUB)
        columns = [whole(here[:, base + v : base + v + 1]) for v in range(SUB)]
        d = {(u, v): whole(columns[v][u : u + 1, :]) for u in range(SUB) for v in range(u + 1)}
        l, r = {}, []
        for u in range(SUB):
            r.append(lax.rsqrt(d[u, u]))
            for v in range(u + 1, SUB):
                l[v, u] = d[v, u] * r[u]
            for v in range(u + 1, SUB):
                for w in range(v, SUB):
                    d[w, v] = d[w, v] - l[w, u] * l[v, u]
        start = jnp.where(inside, (lane - base == row).astype(F32), here)
        y = []
        for u in range(SUB):
            total = whole(start[u : u + 1, :])
            for w in range(u):
                total = total - l[u, w] * y[w]
            y.append(total * r[u])
        tile = y[0]
        for u in range(1, SUB):
            tile = jnp.where(row == u, y[u], tile)
        done.append(jnp.where(lane <= row + base, tile, 0.0))
        if t + 1 < count:
            v = [None] * SUB
            for u in reversed(range(SUB)):
                total = y[u]
                for w in range(u + 1, SUB):
                    total = total - l[w, u] * v[w]
                v[u] = total * r[u]
            for i in range(t + 1, count):
                total = jnp.where(inside, 0.0, tiles[i])
                for u in range(SUB):
                    total = total - whole(tiles[i][:, base + u : base + u + 1]) * v[u]
                tiles[i] = total
    return done


def final_kernel(scale, column, mine_ref, other_ref, m_ref, wg_ref, factors_ref, upper_ref, s_ref, x_ref):
    rows = mine_ref.shape[0]
    blocks = m_ref.shape[0] // rows
    wide = blocks * LANES
    place = column[0]
    n = LANES
    count = n // SUB

    s_ref[0] = wg_ref[0:n, wide : wide + n]
    s_ref[1] = wg_ref[n : 2 * n, wide + n : wide + 2 * n]
    cross = wg_ref[0:n, wide + n : wide + 2 * n]

    def turn(step, carry):
        tiles = lower_inverse([s_ref[step, SUB * t : SUB * (t + 1), :] for t in range(count)])
        for t in range(count):
            x_ref[step, SUB * t : SUB * (t + 1), :] = tiles[t]

        @pl.when(step == 0)
        def _():
            r12 = dot6(x_ref[0], cross)
            s_ref[1] = s_ref[1] - dot6(r12, r12, ((0,), (0,)))
            s_ref[0] = dot6(r12, x_ref[0], ((0,), (0,)))

        return carry

    lax.fori_loop(0, 2, turn, 0)
    x21 = -dot6(x_ref[1], s_ref[0])
    inverse = jnp.concatenate(
        [
            jnp.concatenate([x_ref[0], jnp.zeros((n, n), F32)], axis=1),
            jnp.concatenate([x21, x_ref[1]], axis=1),
        ],
        axis=0,
    )
    turned = inverse.T
    inverse_split, turned_split = split(inverse), split(turned)
    swapped = lax.rem(place, 2) == 1
    mine, other = mine_ref[...], other_ref[...]
    panels = split(
        jnp.concatenate([jnp.where(swapped, other, mine), jnp.where(swapped, mine, other)], axis=1)
    )
    owner = place < 2
    lead = jnp.where(place == 0, turned[:, 0:n], turned[:, n : 2 * n]) * (-scale)
    for k in range(0, blocks, 2):
        coef = dot3(inverse_split, split(wg_ref[:, k * n : (k + 2) * n]))
        for j in range(2):
            upper_ref[pl.ds(k + j, 2 * n, stride=blocks), :] = coef[:, j * n : (j + 1) * n] * (1.0 / scale)
        weights = dot3(turned_split, split(coef))
        left = m_ref[pl.ds(k, rows, stride=blocks), :]
        right = m_ref[pl.ds(k + 1, rows, stride=blocks), :]
        if k == 0:
            weights = jnp.concatenate([jnp.where(owner, lead, weights[:, 0:n]), weights[:, n : 2 * n]], axis=1)
            left = jnp.where(owner, 0.0, left)
        change = dot3(panels, split(weights))
        factors_ref[pl.ds(k, rows, stride=blocks), :] = left - change[:, 0:n]
        factors_ref[pl.ds(k + 1, rows, stride=blocks), :] = right - change[:, n : 2 * n]


VMEM_LIMIT = 56 * 2**20
IN_VMEM = pl.BlockSpec(memory_space=pltpu.VMEM)
IN_SMEM = pl.BlockSpec(memory_space=pltpu.SMEM)


def gram(core, mine, other, m2):
    rows = mine.shape[0]
    blocks = m2.shape[0] // rows
    return pl.pallas_call(
        gram_kernel,
        out_shape=jax.ShapeDtypeStruct((2 * LANES, (blocks + 2) * LANES), F32),
        in_specs=[IN_SMEM, IN_VMEM, IN_VMEM, IN_VMEM],
        out_specs=IN_VMEM,
        compiler_params=pltpu.CompilerParams(vmem_limit_bytes=VMEM_LIMIT),
        name="gram",
    )(core, mine, other, m2)


def finish(scale, column, mine, other, m2, wg):
    rows = mine.shape[0]
    blocks = m2.shape[0] // rows
    return pl.pallas_call(
        functools.partial(final_kernel, scale),
        out_shape=(
            jax.ShapeDtypeStruct(m2.shape, F32),
            jax.ShapeDtypeStruct((2 * LANES * blocks, LANES), F32),
        ),
        in_specs=[IN_SMEM, IN_VMEM, IN_VMEM, IN_VMEM, IN_VMEM],
        out_specs=(IN_VMEM, IN_VMEM),
        scratch_shapes=[pltpu.VMEM((2, LANES, LANES), F32), pltpu.VMEM((2, LANES, LANES), F32)],
        compiler_params=pltpu.CompilerParams(vmem_limit_bytes=VMEM_LIMIT),
        name="finish",
    )(column, mine, other, m2, wg)


def both_cores(pairs):
    return [(2 * a + c, 2 * b + c) for a, b in pairs for c in range(2)]


def spread_panels(lead):
    chip = lax.axis_index("col") // 2
    send = lambda x, pairs: lax.ppermute(x, "col", both_cores(pairs))
    far = send(lead, [(0, 3)]), send(lead, [(0, 5)])
    held = jnp.where(chip == 0, lead, 0.0) + far[0] + far[1]
    near = send(held, [(0, 1), (3, 4), (5, 6)]), send(held, [(0, 7), (3, 2)])
    mine = held + near[0] + near[1]
    other = lax.ppermute(mine, "col", [(i, i ^ 1) for i in range(16)])
    return mine, other


def total_over_rows(part):
    size = lax.axis_size("row")
    height, width = part.shape
    piece = height // size
    got = lax.all_to_all(part, "row", 0, 0, tiled=True)
    mine = jnp.sum(got.reshape(size, piece, width), axis=0)
    repeated = jnp.broadcast_to(mine[None], (size, piece, width)).reshape(height, width)
    return lax.all_to_all(repeated, "row", 0, 0, tiled=True)


def shards(matrix):
    rows, blocks, lanes = matrix.shape
    scale = math.sqrt(rows * lax.axis_size("row"))
    m2 = matrix.reshape(rows * blocks, lanes)
    column = lax.axis_index("col").astype(jnp.int32).reshape(1)
    mine, other = spread_panels(matrix[:, 0, :])
    wg = total_over_rows(gram(lax.rem(column, 2), mine, other, m2))
    factors, upper = finish(scale, column, mine, other, m2, wg)
    return factors.reshape(matrix.shape), upper.reshape(2 * LANES, blocks, lanes)


def solution(mesh):
    in_specs = (P("row", None, "col"),)
    out_specs = (P("row", None, "col"), P(None, None, "col"))
    return jax.shard_map(shards, mesh=mesh, in_specs=in_specs, out_specs=out_specs, check_vma=False)
```

```python
import functools
import math

import jax
import jax.numpy as jnp
from jax import lax
from jax.experimental import pallas as pl
from jax.experimental.pallas import tpu as pltpu
from jax.sharding import PartitionSpec as P

F32 = jnp.float32
BF16 = jnp.bfloat16
HIGHEST = lax.Precision.HIGHEST
LANES = 128
SUB = 8
RANKS = 16
BUDGET = dict(gram=16, halves=50, wide=32, total=16, factor=16, basis=24, finish=54)


def split(x):
    high = x.astype(BF16)
    low = (x - high.astype(F32)).astype(BF16)
    return high, low


def dot3(a, b):
    left = jnp.concatenate([a[0], a[0], a[1]], axis=1)
    right = jnp.concatenate([b[0], b[1], b[0]], axis=0)
    return jnp.dot(left, right, preferred_element_type=F32)


def dot6(a, b, dims=((1,), (0,))):
    return lax.dot_general(a, b, (dims, ((), ())), precision=HIGHEST, preferred_element_type=F32)


def panels_of(second_core, mine_ref, other_ref):
    mine, other = mine_ref[...], other_ref[...]
    return jnp.concatenate(
        [jnp.where(second_core, other, mine), jnp.where(second_core, mine, other)], axis=1
    )


def gram_kernel(column, mine_ref, other_ref, out_ref):
    panels = panels_of(lax.rem(column[0], 2) == 1, mine_ref, other_ref)
    out_ref[...] = dot6(panels.T, panels)


def halves_kernel(column, m_ref, high_ref, low_ref):
    blocks = m_ref.shape[0] // high_ref.shape[0]
    for k in range(blocks):
        here = slice(k * LANES, (k + 1) * LANES)
        high_ref[:, here], low_ref[:, here] = split(m_ref[pl.ds(k, high_ref.shape[0], stride=blocks), :])


def wide_kernel(column, mine_ref, other_ref, high_ref, low_ref, out_ref):
    left = split(panels_of(lax.rem(column[0], 2) == 1, mine_ref, other_ref).T)
    step = 2 * LANES
    for k in range(0, out_ref.shape[1], step):
        here = slice(k, k + step)
        out_ref[:, here] = dot3(left, (high_ref[:, here], low_ref[:, here]))


def total_kernel(column, part_ref, out_ref):
    piece = part_ref.shape[0] // RANKS
    total = part_ref[0:piece, :]
    for r in range(1, RANKS):
        total = total + part_ref[r * piece : (r + 1) * piece, :]
    for r in range(RANKS):
        out_ref[r * piece : (r + 1) * piece, :] = total


def lower_inverse(tiles):
    count = len(tiles)
    tiles = list(tiles)
    lane = lax.broadcasted_iota(jnp.int32, (SUB, LANES), 1)
    row = lax.broadcasted_iota(jnp.int32, (SUB, LANES), 0)
    whole = lambda x: jnp.broadcast_to(x, (SUB, LANES))
    done = []
    for t in range(count):
        base = SUB * t
        here = tiles[t]
        inside = (lane >= base) & (lane < base + SUB)
        columns = [whole(here[:, base + v : base + v + 1]) for v in range(SUB)]
        d = {(u, v): whole(columns[v][u : u + 1, :]) for u in range(SUB) for v in range(u + 1)}
        l, r = {}, []
        for u in range(SUB):
            r.append(lax.rsqrt(d[u, u]))
            for v in range(u + 1, SUB):
                l[v, u] = d[v, u] * r[u]
            for v in range(u + 1, SUB):
                for w in range(v, SUB):
                    d[w, v] = d[w, v] - l[w, u] * l[v, u]
        start = jnp.where(inside, (lane - base == row).astype(F32), here)
        y = []
        for u in range(SUB):
            total = whole(start[u : u + 1, :])
            for w in range(u):
                total = total - l[u, w] * y[w]
            y.append(total * r[u])
        tile = y[0]
        for u in range(1, SUB):
            tile = jnp.where(row == u, y[u], tile)
        done.append(jnp.where(lane <= row + base, tile, 0.0))
        if t + 1 < count:
            v = [None] * SUB
            for u in reversed(range(SUB)):
                total = y[u]
                for w in range(u + 1, SUB):
                    total = total - l[w, u] * v[w]
                v[u] = total * r[u]
            for i in range(t + 1, count):
                total = jnp.where(inside, 0.0, tiles[i])
                for u in range(SUB):
                    total = total - whole(tiles[i][:, base + u : base + u + 1]) * v[u]
                tiles[i] = total
    return done


def factor_kernel(column, g_ref, x_ref, s_ref):
    n = LANES
    count = n // SUB
    s_ref[0] = g_ref[0:n, 0:n]
    s_ref[1] = g_ref[n : 2 * n, n : 2 * n]

    def turn(step, carry):
        tiles = lower_inverse([s_ref[step, SUB * t : SUB * (t + 1), :] for t in range(count)])
        for t in range(count):
            x_ref[step, SUB * t : SUB * (t + 1), :] = tiles[t]

        @pl.when(step == 0)
        def _():
            r12 = dot6(x_ref[0], g_ref[0:n, n : 2 * n])
            s_ref[1] = s_ref[1] - dot6(r12, r12, ((0,), (0,)))
            s_ref[0] = dot6(r12, x_ref[0], ((0,), (0,)))

        return carry

    lax.fori_loop(0, 2, turn, 0)
    x_ref[2] = -dot6(x_ref[1], s_ref[0])


def whole_inverse(x_ref):
    n = LANES
    return jnp.concatenate(
        [
            jnp.concatenate([x_ref[0], jnp.zeros((n, n), F32)], axis=1),
            jnp.concatenate([x_ref[2], x_ref[1]], axis=1),
        ],
        axis=0,
    )


def basis_kernel(column, mine_ref, other_ref, x_ref, high_ref, low_ref):
    panels = panels_of(lax.rem(column[0], 2) == 1, mine_ref, other_ref)
    high_ref[...], low_ref[...] = split(dot3(split(panels), split(whole_inverse(x_ref).T)))


def final_kernel(
    scale, column, high_ref, low_ref, m_ref, w_ref, x_ref, factors_ref, upper_ref, coef_ref, ch_ref, cl_ref
):
    rows = high_ref.shape[0]
    blocks = m_ref.shape[0] // rows
    place = column[0]
    n = LANES
    owner = place < 2
    turn = pl.program_id(0)

    @pl.when(turn == 0)
    def _():
        inverse = split(whole_inverse(x_ref))
        unit = lax.broadcasted_iota(jnp.int32, (2 * n, n), 0) == lax.broadcasted_iota(jnp.int32, (2 * n, n), 1) + place * n
        unit = jnp.where(unit, -scale, 0.0)
        for k in range(0, blocks, 2):
            here = slice(k * n, (k + 2) * n)
            coef = dot3(inverse, split(w_ref[:, here]))
            coef_ref[:, here] = coef * (1.0 / scale)
            if k == 0:
                coef = jnp.concatenate([jnp.where(owner, unit, coef[:, 0:n]), coef[:, n : 2 * n]], axis=1)
            ch_ref[:, here], cl_ref[:, here] = split(coef)

    basis = high_ref[...], low_ref[...]
    for k in range(0, blocks, 2):
        here = slice(k * n, (k + 2) * n)
        change = dot3(basis, (ch_ref[:, here], cl_ref[:, here]))
        left = m_ref[pl.ds(k, rows, stride=blocks), :]
        if k == 0:
            left = jnp.where(owner, 0.0, left)
        factors_ref[pl.ds(k, rows, stride=blocks), :] = left - change[:, 0:n]
        factors_ref[pl.ds(k + 1, rows, stride=blocks), :] = (
            m_ref[pl.ds(k + 1, rows, stride=blocks), :] - change[:, n : 2 * n]
        )
    some = upper_ref.shape[0] // blocks
    for k in range(blocks):
        upper_ref[pl.ds(k, some, stride=blocks), :] = coef_ref[
            pl.ds(pl.multiple_of(turn * some, some), some), k * n : (k + 1) * n
        ]


IN_SMEM = pl.BlockSpec(memory_space=pltpu.SMEM)


def by_rows(array, steps):
    return pl.BlockSpec((array.shape[0] // steps, array.shape[1]), lambda i: (i, 0))


def fixed(array):
    return pl.BlockSpec(array.shape, lambda i: (0,) * len(array.shape))


def kernel_call(body, name, micros, steps, operands, out_shape, row_split, scratch=()):
    specs = [by_rows(x, steps) if s else fixed(x) for x, s in zip((*operands[1:], *out_shape), row_split)]
    return pl.pallas_call(
        body,
        grid=(steps,),
        out_shape=out_shape,
        in_specs=[IN_SMEM] + specs[: len(operands) - 1],
        out_specs=tuple(specs[len(operands) - 1 :]),
        scratch_shapes=list(scratch),
        compiler_params=pltpu.CompilerParams(vmem_limit_bytes=BUDGET[name] * 2**20),
        cost_estimate=pl.CostEstimate(flops=micros * 10**9, bytes_accessed=micros * 10**6, transcendentals=0),
        name=name,
    )(*operands)


def shape(*dims):
    return jax.ShapeDtypeStruct(dims, F32)


def both_cores(pairs):
    return [(2 * a + c, 2 * b + c) for a, b in pairs for c in range(2)]


def send(x, pairs):
    return lax.ppermute(x, "col", both_cores(pairs))


def spread_far(x, chip):
    far = send(x, [(0, 3)]), send(x, [(0, 5)])
    return jnp.where(chip == 0, x, 0.0) + far[0] + far[1]


def spread_near(x):
    return send(x, [(0, 1), (3, 4), (5, 6)]), send(x, [(0, 7), (3, 2)])


def total(column, part):
    return kernel_call(total_kernel, "total", 1, 1, (column, part), (shape(*part.shape),), (0, 0))[0]


def exchange(x):
    return lax.all_to_all(x, "row", 0, 0, tiled=True)


def shards(matrix):
    rows, blocks, lanes = matrix.shape
    size = lax.axis_size("row")
    scale = math.sqrt(rows * size)
    steps = 4
    m2 = matrix.reshape(rows * blocks, lanes)
    column = lax.axis_index("col").astype(jnp.int32).reshape(1)
    chip = lax.axis_index("col") // 2
    lead = matrix[:, 0, :]
    n = 2 * lanes
    partner = lax.ppermute(lead, "col", [(0, 1), (1, 0)])
    (part,) = kernel_call(gram_kernel, "gram", 3, 1, (column, lead, partner), (shape(n, n),), (0, 0, 0))
    half = jax.ShapeDtypeStruct((rows, blocks * lanes), BF16)
    later, part = lax.optimization_barrier((column, part))
    m_high, m_low = kernel_call(halves_kernel, "halves", 4, steps, (later, m2), (half, half), (1, 1, 1))
    part = exchange(part)
    far = send(lead, [(0, 3)]), send(lead, [(0, 5)])
    far, _, _ = lax.optimization_barrier((far, m_high, m_low))
    held = jnp.where(chip == 0, lead, 0.0) + far[0] + far[1]
    part, held = lax.optimization_barrier((part, held))
    near = spread_near(held)
    gram = exchange(total(column, part))
    near, gram = lax.optimization_barrier((near, gram))
    mine = held + near[0] + near[1]
    other = lax.ppermute(mine, "col", [(i, i ^ 1) for i in range(16)])
    (wide,) = kernel_call(
        wide_kernel, "wide", 6, 1, (column, mine, other, m_high, m_low), (shape(n, blocks * lanes),), (0,) * 5
    )
    gram, wide = lax.optimization_barrier((gram, wide))
    wide = exchange(wide)
    (factor,) = kernel_call(
        factor_kernel, "factor", 12, 1, (column, gram), (shape(3, lanes, lanes),), (0, 0),
        scratch=[pltpu.VMEM((2, lanes, lanes), F32)],
    )
    _, wide = lax.optimization_barrier((factor, wide))
    factor_far = spread_far(factor, chip)
    wide = exchange(total(column, wide))
    near = spread_near(factor_far)
    factor = factor_far + near[0] + near[1]
    half = jax.ShapeDtypeStruct((rows, n), BF16)
    high, low = kernel_call(
        basis_kernel, "basis", 2, 1, (column, mine, other, factor), (half, half), (0, 0, 0, 0, 0)
    )
    factors, upper = kernel_call(
        functools.partial(final_kernel, scale), "finish", 6, steps,
        (column, high, low, m2, wide, factor), (shape(*m2.shape), shape(n * blocks, lanes)),
        (1, 1, 1, 0, 0, 1, 1), scratch=[pltpu.VMEM((n, blocks * lanes), t) for t in (F32, BF16, BF16)],
    )
    return factors.reshape(matrix.shape), upper.reshape(n, blocks, lanes)


def solution(mesh):
    in_specs = (P("row", None, "col"),)
    out_specs = (P("row", None, "col"), P(None, None, "col"))
    return jax.shard_map(shards, mesh=mesh, in_specs=in_specs, out_specs=out_specs, check_vma=False)
```

```python
import functools
import math

import jax
import jax.numpy as jnp
from jax import lax
from jax.experimental import pallas as pl
from jax.experimental.pallas import tpu as pltpu
from jax.sharding import PartitionSpec as P

F32 = jnp.float32
BF16 = jnp.bfloat16
HIGHEST = lax.Precision.HIGHEST
LANES = 128
SUB = 8
RANKS = 16
BUDGET = dict(gram=16, halves=60, wide=50, total=16, factor=16, basis=24, finish=60)


def split(x):
    high = x.astype(BF16)
    low = (x - high.astype(F32)).astype(BF16)
    return high, low


def dot3(a, b):
    left = jnp.concatenate([a[0], a[0], a[1]], axis=1)
    right = jnp.concatenate([b[0], b[1], b[0]], axis=0)
    return jnp.dot(left, right, preferred_element_type=F32)


def dot6(a, b, dims=((1,), (0,))):
    return lax.dot_general(a, b, (dims, ((), ())), precision=HIGHEST, preferred_element_type=F32)


def panels_of(second_core, mine_ref, other_ref):
    mine, other = mine_ref[...], other_ref[...]
    return jnp.concatenate(
        [jnp.where(second_core, other, mine), jnp.where(second_core, mine, other)], axis=1
    )


def gram_kernel(column, mine_ref, other_ref, out_ref):
    panels = panels_of(lax.rem(column[0], 2) == 1, mine_ref, other_ref)
    out_ref[...] = dot6(panels.T, panels)


def halves_kernel(column, m_ref, high_ref, low_ref):
    blocks = m_ref.shape[0] // high_ref.shape[0]
    for k in range(blocks):
        here = slice(k * LANES, (k + 1) * LANES)
        high_ref[:, here], low_ref[:, here] = split(m_ref[pl.ds(k, high_ref.shape[0], stride=blocks), :])


def wide_kernel(column, mine_ref, other_ref, high_ref, low_ref, out_ref, left_ref):
    @pl.when(pl.program_id(0) == 0)
    def _():
        left_ref[0], left_ref[1] = split(panels_of(lax.rem(column[0], 2) == 1, mine_ref, other_ref).T)

    out_ref[...] = dot3((left_ref[0], left_ref[1]), (high_ref[...], low_ref[...]))


def total_kernel(column, part_ref, out_ref):
    piece = part_ref.shape[0] // RANKS
    total = part_ref[0:piece, :]
    for r in range(1, RANKS):
        total = total + part_ref[r * piece : (r + 1) * piece, :]
    for r in range(RANKS):
        out_ref[r * piece : (r + 1) * piece, :] = total


def lower_inverse(tiles):
    count = len(tiles)
    tiles = list(tiles)
    lane = lax.broadcasted_iota(jnp.int32, (SUB, LANES), 1)
    row = lax.broadcasted_iota(jnp.int32, (SUB, LANES), 0)
    whole = lambda x: jnp.broadcast_to(x, (SUB, LANES))
    done = []
    for t in range(count):
        base = SUB * t
        here = tiles[t]
        inside = (lane >= base) & (lane < base + SUB)
        columns = [whole(here[:, base + v : base + v + 1]) for v in range(SUB)]
        d = {(u, v): whole(columns[v][u : u + 1, :]) for u in range(SUB) for v in range(u + 1)}
        l, r = {}, []
        for u in range(SUB):
            r.append(lax.rsqrt(d[u, u]))
            for v in range(u + 1, SUB):
                l[v, u] = d[v, u] * r[u]
            for v in range(u + 1, SUB):
                for w in range(v, SUB):
                    d[w, v] = d[w, v] - l[w, u] * l[v, u]
        start = jnp.where(inside, (lane - base == row).astype(F32), here)
        y = []
        for u in range(SUB):
            total = whole(start[u : u + 1, :])
            for w in range(u):
                total = total - l[u, w] * y[w]
            y.append(total * r[u])
        tile = y[0]
        for u in range(1, SUB):
            tile = jnp.where(row == u, y[u], tile)
        done.append(jnp.where(lane <= row + base, tile, 0.0))
        if t + 1 < count:
            v = [None] * SUB
            for u in reversed(range(SUB)):
                total = y[u]
                for w in range(u + 1, SUB):
                    total = total - l[w, u] * v[w]
                v[u] = total * r[u]
            for i in range(t + 1, count):
                total = jnp.where(inside, 0.0, tiles[i])
                for u in range(SUB):
                    total = total - whole(tiles[i][:, base + u : base + u + 1]) * v[u]
                tiles[i] = total
    return done


def factor_kernel(column, g_ref, x_ref, s_ref):
    n = LANES
    count = n // SUB
    s_ref[0] = g_ref[0:n, 0:n]
    s_ref[1] = g_ref[n : 2 * n, n : 2 * n]

    def turn(step, carry):
        tiles = lower_inverse([s_ref[step, SUB * t : SUB * (t + 1), :] for t in range(count)])
        for t in range(count):
            x_ref[step, SUB * t : SUB * (t + 1), :] = tiles[t]

        @pl.when(step == 0)
        def _():
            r12 = dot6(x_ref[0], g_ref[0:n, n : 2 * n])
            s_ref[1] = s_ref[1] - dot6(r12, r12, ((0,), (0,)))
            s_ref[0] = dot6(r12, x_ref[0], ((0,), (0,)))

        return carry

    lax.fori_loop(0, 2, turn, 0)
    x_ref[2] = -dot6(x_ref[1], s_ref[0])


def whole_inverse(x_ref):
    n = LANES
    return jnp.concatenate(
        [
            jnp.concatenate([x_ref[0], jnp.zeros((n, n), F32)], axis=1),
            jnp.concatenate([x_ref[2], x_ref[1]], axis=1),
        ],
        axis=0,
    )


def basis_kernel(column, mine_ref, other_ref, x_ref, high_ref, low_ref):
    panels = panels_of(lax.rem(column[0], 2) == 1, mine_ref, other_ref)
    high_ref[...], low_ref[...] = split(dot3(split(panels), split(whole_inverse(x_ref).T)))


def final_kernel(
    scale, chunks, column, high_in, low_in, m_in, w_in, x_in, factors_out, upper_out,
    high_ref, low_ref, m_ref, w_ref, x_ref, up_ref, ch_ref, cl_ref, small_sem, in_sem, out_sem, up_sem,
):
    all_rows = high_ref.shape[0]
    rows = all_rows // chunks
    blocks = m_ref.shape[0] // all_rows
    place = column[0]
    n = LANES
    owner = place < 2
    copy = pltpu.make_async_copy
    piece = lambda i: pl.ds(i * rows * blocks, rows * blocks)
    small = [
        copy(src, dst, small_sem.at[i])
        for i, (src, dst) in enumerate(((x_in, x_ref), (w_in, w_ref), (high_in, high_ref), (low_in, low_ref)))
    ]
    for c in small:
        c.start()
    reads = [copy(m_in.at[piece(i), :], m_ref.at[piece(i), :], in_sem.at[i]) for i in range(chunks)]
    writes = [copy(m_ref.at[piece(i), :], factors_out.at[piece(i), :], out_sem.at[i]) for i in range(chunks)]
    for c in reads:
        c.start()
    small[0].wait()
    inverse = split(whole_inverse(x_ref))
    unit = lax.broadcasted_iota(jnp.int32, (2 * n, n), 0) == lax.broadcasted_iota(jnp.int32, (2 * n, n), 1) + place * n
    unit = jnp.where(unit, -scale, 0.0)
    small[1].wait()
    for k in range(0, blocks, 2):
        here = slice(k * n, (k + 2) * n)
        coef = dot3(inverse, split(w_ref[:, here]))
        for j in range(2):
            up_ref[pl.ds(k + j, 2 * n, stride=blocks), :] = coef[:, j * n : (j + 1) * n] * (1.0 / scale)
        if k == 0:
            coef = jnp.concatenate([jnp.where(owner, unit, coef[:, 0:n]), coef[:, n : 2 * n]], axis=1)
        ch_ref[:, here], cl_ref[:, here] = split(coef)
    upper = copy(up_ref, upper_out, up_sem)
    upper.start()
    small[2].wait()
    small[3].wait()
    for i in range(chunks):
        basis = high_ref[i * rows : (i + 1) * rows, :], low_ref[i * rows : (i + 1) * rows, :]
        reads[i].wait()
        for k in range(0, blocks, 2):
            here = slice(k * n, (k + 2) * n)
            change = dot3(basis, (ch_ref[:, here], cl_ref[:, here]))
            for j in range(2):
                at = pl.ds(i * rows * blocks + k + j, rows, stride=blocks)
                old = m_ref[at, :]
                if k + j == 0:
                    old = jnp.where(owner, 0.0, old)
                m_ref[at, :] = old - change[:, j * n : (j + 1) * n]
        writes[i].start()
    upper.wait()
    for c in writes:
        c.wait()


IN_SMEM = pl.BlockSpec(memory_space=pltpu.SMEM)
ANYWHERE = pl.BlockSpec(memory_space=pl.ANY)


def by_rows(array, steps):
    return pl.BlockSpec((array.shape[0] // steps, array.shape[1]), lambda i: (i, 0))


def by_columns(array, steps):
    return pl.BlockSpec((array.shape[0], array.shape[1] // steps), lambda i: (0, i))


def fixed(array):
    return pl.BlockSpec(array.shape, lambda i: (0,) * len(array.shape))


def kernel_call(body, name, micros, steps, operands, out_shape, row_split, scratch=()):
    specs = [by_rows(x, steps) if s == 1 else ANYWHERE if s == 2 else by_columns(x, steps) if s == 3 else fixed(x) for x, s in zip((*operands[1:], *out_shape), row_split)]
    return pl.pallas_call(
        body,
        grid=(steps,),
        out_shape=out_shape,
        in_specs=[IN_SMEM] + specs[: len(operands) - 1],
        out_specs=tuple(specs[len(operands) - 1 :]),
        scratch_shapes=list(scratch),
        compiler_params=pltpu.CompilerParams(vmem_limit_bytes=BUDGET[name] * 2**20),
        cost_estimate=pl.CostEstimate(flops=micros * 10**9, bytes_accessed=micros * 10**6, transcendentals=0),
        name=name,
    )(*operands)


def shape(*dims):
    return jax.ShapeDtypeStruct(dims, F32)


def both_cores(pairs):
    return [(2 * a + c, 2 * b + c) for a, b in pairs for c in range(2)]


def by_core(first, second):
    return [(2 * a, 2 * b) for a, b in first] + [(2 * a + 1, 2 * b + 1) for a, b in second]


def send(x, pairs):
    return lax.ppermute(x, "col", both_cores(pairs))


def spread_far(x, chip):
    far = send(x, [(0, 3)]), send(x, [(0, 5)])
    return jnp.where(chip == 0, x, 0.0) + far[0] + far[1]


def spread_near(x):
    return send(x, [(0, 1), (3, 4), (5, 6)]), send(x, [(0, 7), (3, 2)])


def total(column, part, micros=1):
    return kernel_call(total_kernel, "total", micros, 1, (column, part), (shape(*part.shape),), (0, 0))[0]


def exchange(x):
    return lax.all_to_all(x, "row", 0, 0, tiled=True)


def shards(matrix):
    rows, blocks, lanes = matrix.shape
    size = lax.axis_size("row")
    scale = math.sqrt(rows * size)
    steps = 4
    m2 = matrix.reshape(rows * blocks, lanes)
    column = lax.axis_index("col").astype(jnp.int32).reshape(1)
    chip = lax.axis_index("col") // 2
    lead = matrix[:, 0, :]
    n = 2 * lanes
    partner = lax.ppermute(lead, "col", [(0, 1), (1, 0)])
    (part,) = kernel_call(gram_kernel, "gram", 3, 1, (column, lead, partner), (shape(n, n),), (0, 0, 0))
    half = jax.ShapeDtypeStruct((rows, blocks * lanes), BF16)
    lead, part = lax.optimization_barrier((lead, part))
    hop = lambda x, first, second: lax.ppermute(x, "col", by_core(first, second))
    part = exchange(part)
    first = hop(lead, [(0, 3)], [(0, 5)])
    held = jnp.where(chip == 0, lead, 0.0) + first
    part, _ = lax.optimization_barrier((part, held))
    near = hop(held, [(0, 7), (3, 4)], [(0, 1), (5, 6)]), hop(held, [(3, 2)], [(5, 4)])
    summed = total(column, part, 30)
    near, summed = lax.optimization_barrier((near, summed))
    more = held + near[0] + near[1]
    gram = exchange(summed)
    later, _ = lax.optimization_barrier((column, more))
    m_high, m_low = kernel_call(halves_kernel, "halves", 4, steps, (later, m2), (half, half), (1, 1, 1))
    last = hop(more, [(2, 1), (4, 5), (7, 6)], [(6, 7), (4, 3), (1, 2)])
    last, _, _ = lax.optimization_barrier((last, m_high, m_low))
    last, gram = lax.optimization_barrier((last, gram))
    mine = more + last
    other = lax.ppermute(mine, "col", [(i, i ^ 1) for i in range(16)])
    (wide,) = kernel_call(
        wide_kernel, "wide", 6, steps, (column, mine, other, m_high, m_low), (shape(n, blocks * lanes),),
        (0, 0, 3, 3, 3), scratch=[pltpu.VMEM((2, n, rows), BF16)],
    )
    gram, wide = lax.optimization_barrier((gram, wide))
    wide = exchange(wide)
    (factor,) = kernel_call(
        factor_kernel, "factor", 12, 1, (column, gram), (shape(3, lanes, lanes),), (0, 0),
        scratch=[pltpu.VMEM((2, lanes, lanes), F32)],
    )
    _, wide = lax.optimization_barrier((factor, wide))
    factor_far = spread_far(factor, chip)
    wide = exchange(total(column, wide))
    near = spread_near(factor_far)
    factor = factor_far + near[0] + near[1]
    half = jax.ShapeDtypeStruct((rows, n), BF16)
    high, low = kernel_call(
        basis_kernel, "basis", 2, 1, (column, mine, other, factor), (half, half), (0, 0, 0, 0, 0)
    )
    chunks = 4
    dma = pltpu.SemaphoreType.DMA
    factors, upper = kernel_call(
        functools.partial(final_kernel, scale, chunks), "finish", 6, 1,
        (column, high, low, m2, wide, factor), (shape(*m2.shape), shape(n * blocks, lanes)), (2,) * 7,
        scratch=[
            pltpu.VMEM((rows, n), BF16), pltpu.VMEM((rows, n), BF16), pltpu.VMEM(m2.shape, F32),
            pltpu.VMEM((n, blocks * lanes), F32), pltpu.VMEM((3, lanes, lanes), F32),
            pltpu.VMEM((n * blocks, lanes), F32), pltpu.VMEM((n, blocks * lanes), BF16),
            pltpu.VMEM((n, blocks * lanes), BF16), dma((4,)), dma((chunks,)), dma((chunks,)), dma(()),
        ],
    )
    return factors.reshape(matrix.shape), upper.reshape(n, blocks, lanes)


def solution(mesh):
    in_specs = (P("row", None, "col"),)
    out_specs = (P("row", None, "col"), P(None, None, "col"))
    return jax.shard_map(shards, mesh=mesh, in_specs=in_specs, out_specs=out_specs, check_vma=False)
```

```python
import functools
import math

import jax
import jax.numpy as jnp
from jax import lax
from jax.experimental import pallas as pl
from jax.experimental.pallas import tpu as pltpu
from jax.sharding import PartitionSpec as P

F32 = jnp.float32
BF16 = jnp.bfloat16
HIGHEST = lax.Precision.HIGHEST
LANES = 128
SUB = 8
RANKS = 16
BUDGET = dict(gram=16, halves=60, wide=32, total=16, factor=16, basis=24, finish=60)


def split(x):
    high = x.astype(BF16)
    low = (x - high.astype(F32)).astype(BF16)
    return high, low


def dot3(a, b):
    left = jnp.concatenate([a[0], a[0], a[1]], axis=1)
    right = jnp.concatenate([b[0], b[1], b[0]], axis=0)
    return jnp.dot(left, right, preferred_element_type=F32)


def dot6(a, b, dims=((1,), (0,))):
    return lax.dot_general(a, b, (dims, ((), ())), precision=HIGHEST, preferred_element_type=F32)


def panels_of(second_core, mine_ref, other_ref):
    mine, other = mine_ref[...], other_ref[...]
    return jnp.concatenate(
        [jnp.where(second_core, other, mine), jnp.where(second_core, mine, other)], axis=1
    )


def gram_kernel(column, mine_ref, other_ref, out_ref):
    panels = panels_of(lax.rem(column[0], 2) == 1, mine_ref, other_ref)
    out_ref[...] = dot6(panels.T, panels)


def halves_kernel(column, m_ref, high_ref, low_ref):
    blocks = m_ref.shape[0] // high_ref.shape[0]
    for k in range(blocks):
        here = slice(k * LANES, (k + 1) * LANES)
        high_ref[:, here], low_ref[:, here] = split(m_ref[pl.ds(k, high_ref.shape[0], stride=blocks), :])


def wide_kernel(column, mine_ref, other_ref, high_ref, low_ref, out_ref):
    left = split(panels_of(lax.rem(column[0], 2) == 1, mine_ref, other_ref).T)
    step = 2 * LANES
    for k in range(0, out_ref.shape[1], step):
        here = slice(k, k + step)
        out_ref[:, here] = dot3(left, (high_ref[:, here], low_ref[:, here]))


def total_kernel(column, part_ref, out_ref):
    piece = part_ref.shape[0] // RANKS
    total = part_ref[0:piece, :]
    for r in range(1, RANKS):
        total = total + part_ref[r * piece : (r + 1) * piece, :]
    for r in range(RANKS):
        out_ref[r * piece : (r + 1) * piece, :] = total


def lower_inverse(tiles):
    count = len(tiles)
    tiles = list(tiles)
    lane = lax.broadcasted_iota(jnp.int32, (SUB, LANES), 1)
    row = lax.broadcasted_iota(jnp.int32, (SUB, LANES), 0)
    whole = lambda x: jnp.broadcast_to(x, (SUB, LANES))
    done = []
    for t in range(count):
        base = SUB * t
        here = tiles[t]
        inside = (lane >= base) & (lane < base + SUB)
        columns = [whole(here[:, base + v : base + v + 1]) for v in range(SUB)]
        d = {(u, v): whole(columns[v][u : u + 1, :]) for u in range(SUB) for v in range(u + 1)}
        l, r = {}, []
        for u in range(SUB):
            r.append(lax.rsqrt(d[u, u]))
            for v in range(u + 1, SUB):
                l[v, u] = d[v, u] * r[u]
            for v in range(u + 1, SUB):
                for w in range(v, SUB):
                    d[w, v] = d[w, v] - l[w, u] * l[v, u]
        start = jnp.where(inside, (lane - base == row).astype(F32), here)
        y = []
        for u in range(SUB):
            total = whole(start[u : u + 1, :])
            for w in range(u):
                total = total - l[u, w] * y[w]
            y.append(total * r[u])
        tile = y[0]
        for u in range(1, SUB):
            tile = jnp.where(row == u, y[u], tile)
        done.append(jnp.where(lane <= row + base, tile, 0.0))
        if t + 1 < count:
            v = [None] * SUB
            for u in reversed(range(SUB)):
                total = y[u]
                for w in range(u + 1, SUB):
                    total = total - l[w, u] * v[w]
                v[u] = total * r[u]
            for i in range(t + 1, count):
                total = jnp.where(inside, 0.0, tiles[i])
                for u in range(SUB):
                    total = total - whole(tiles[i][:, base + u : base + u + 1]) * v[u]
                tiles[i] = total
    return done


def factor_kernel(column, g_ref, x_ref, s_ref):
    n = LANES
    count = n // SUB
    s_ref[0] = g_ref[0:n, 0:n]
    s_ref[1] = g_ref[n : 2 * n, n : 2 * n]

    def turn(step, carry):
        tiles = lower_inverse([s_ref[step, SUB * t : SUB * (t + 1), :] for t in range(count)])
        for t in range(count):
            x_ref[step, SUB * t : SUB * (t + 1), :] = tiles[t]

        @pl.when(step == 0)
        def _():
            r12 = dot6(x_ref[0], g_ref[0:n, n : 2 * n])
            s_ref[1] = s_ref[1] - dot6(r12, r12, ((0,), (0,)))
            s_ref[0] = dot6(r12, x_ref[0], ((0,), (0,)))

        return carry

    lax.fori_loop(0, 2, turn, 0)
    x_ref[2] = -dot6(x_ref[1], s_ref[0])


def whole_inverse(x_ref):
    n = LANES
    return jnp.concatenate(
        [
            jnp.concatenate([x_ref[0], jnp.zeros((n, n), F32)], axis=1),
            jnp.concatenate([x_ref[2], x_ref[1]], axis=1),
        ],
        axis=0,
    )


def basis_kernel(column, mine_ref, other_ref, x_ref, high_ref, low_ref):
    panels = panels_of(lax.rem(column[0], 2) == 1, mine_ref, other_ref)
    high_ref[...], low_ref[...] = split(dot3(split(panels), split(whole_inverse(x_ref).T)))


def final_kernel(
    scale, chunks, column, high_in, low_in, m_in, w_in, x_in, factors_out, upper_out,
    high_ref, low_ref, m_ref, w_ref, x_ref, up_ref, ch_ref, cl_ref, small_sem, in_sem, out_sem, up_sem,
):
    all_rows = high_ref.shape[0]
    rows = all_rows // chunks
    blocks = m_ref.shape[0] // all_rows
    place = column[0]
    n = LANES
    owner = place < 2
    copy = pltpu.make_async_copy
    piece = lambda i: pl.ds(i * rows * blocks, rows * blocks)
    small = [
        copy(src, dst, small_sem.at[i])
        for i, (src, dst) in enumerate(((x_in, x_ref), (w_in, w_ref), (high_in, high_ref), (low_in, low_ref)))
    ]
    for c in small:
        c.start()
    reads = [copy(m_in.at[piece(i), :], m_ref.at[piece(i), :], in_sem.at[i]) for i in range(chunks)]
    writes = [copy(m_ref.at[piece(i), :], factors_out.at[piece(i), :], out_sem.at[i]) for i in range(chunks)]
    for c in reads:
        c.start()
    small[0].wait()
    inverse = split(whole_inverse(x_ref))
    unit = lax.broadcasted_iota(jnp.int32, (2 * n, n), 0) == lax.broadcasted_iota(jnp.int32, (2 * n, n), 1) + place * n
    unit = jnp.where(unit, -scale, 0.0)
    small[1].wait()
    for k in range(0, blocks, 2):
        here = slice(k * n, (k + 2) * n)
        coef = dot3(inverse, split(w_ref[:, here]))
        for j in range(2):
            up_ref[pl.ds(k + j, 2 * n, stride=blocks), :] = coef[:, j * n : (j + 1) * n] * (1.0 / scale)
        if k == 0:
            coef = jnp.concatenate([jnp.where(owner, unit, coef[:, 0:n]), coef[:, n : 2 * n]], axis=1)
        ch_ref[:, here], cl_ref[:, here] = split(coef)
    upper = copy(up_ref, upper_out, up_sem)
    upper.start()
    small[2].wait()
    small[3].wait()
    for i in range(chunks):
        basis = high_ref[i * rows : (i + 1) * rows, :], low_ref[i * rows : (i + 1) * rows, :]
        reads[i].wait()
        for k in range(0, blocks, 2):
            here = slice(k * n, (k + 2) * n)
            change = dot3(basis, (ch_ref[:, here], cl_ref[:, here]))
            for j in range(2):
                at = pl.ds(i * rows * blocks + k + j, rows, stride=blocks)
                old = m_ref[at, :]
                if k + j == 0:
                    old = jnp.where(owner, 0.0, old)
                m_ref[at, :] = old - change[:, j * n : (j + 1) * n]
        writes[i].start()
    upper.wait()
    for c in writes:
        c.wait()


IN_SMEM = pl.BlockSpec(memory_space=pltpu.SMEM)
ANYWHERE = pl.BlockSpec(memory_space=pl.ANY)


def by_rows(array, steps):
    return pl.BlockSpec((array.shape[0] // steps, array.shape[1]), lambda i: (i, 0))


def fixed(array):
    return pl.BlockSpec(array.shape, lambda i: (0,) * len(array.shape))


def kernel_call(body, name, micros, steps, operands, out_shape, row_split, scratch=()):
    specs = [by_rows(x, steps) if s == 1 else ANYWHERE if s == 2 else fixed(x) for x, s in zip((*operands[1:], *out_shape), row_split)]
    return pl.pallas_call(
        body,
        grid=(steps,),
        out_shape=out_shape,
        in_specs=[IN_SMEM] + specs[: len(operands) - 1],
        out_specs=tuple(specs[len(operands) - 1 :]),
        scratch_shapes=list(scratch),
        compiler_params=pltpu.CompilerParams(vmem_limit_bytes=BUDGET[name] * 2**20),
        cost_estimate=pl.CostEstimate(flops=micros * 10**9, bytes_accessed=micros * 10**6, transcendentals=0),
        name=name,
    )(*operands)


def shape(*dims):
    return jax.ShapeDtypeStruct(dims, F32)


def both_cores(pairs):
    return [(2 * a + c, 2 * b + c) for a, b in pairs for c in range(2)]


def send(x, pairs):
    return lax.ppermute(x, "col", both_cores(pairs))


def spread_far(x, chip):
    far = send(x, [(0, 3)]), send(x, [(0, 5)])
    return jnp.where(chip == 0, x, 0.0) + far[0] + far[1]


def spread_near(x):
    return send(x, [(0, 1), (3, 4), (5, 6)]), send(x, [(0, 7), (3, 2)])


def total(column, part, micros=1):
    return kernel_call(total_kernel, "total", micros, 1, (column, part), (shape(*part.shape),), (0, 0))[0]


def exchange(x):
    return lax.all_to_all(x, "row", 0, 0, tiled=True)


def shards(matrix):
    rows, blocks, lanes = matrix.shape
    size = lax.axis_size("row")
    scale = math.sqrt(rows * size)
    steps = 4
    m2 = matrix.reshape(rows * blocks, lanes)
    column = lax.axis_index("col").astype(jnp.int32).reshape(1)
    chip = lax.axis_index("col") // 2
    lead = matrix[:, 0, :]
    n = 2 * lanes
    partner = lax.ppermute(lead, "col", [(0, 1), (1, 0)])
    (part,) = kernel_call(gram_kernel, "gram", 3, 1, (column, lead, partner), (shape(n, n),), (0, 0, 0))
    half = jax.ShapeDtypeStruct((rows, blocks * lanes), BF16)
    later, raw = lax.optimization_barrier((column, part))
    m_high, m_low = kernel_call(halves_kernel, "halves", 4, steps, (later, m2), (half, half), (1, 1, 1))
    far = send(lead, [(0, 3)]), send(lead, [(0, 5)])
    far, _, _, _ = lax.optimization_barrier((far, m_high, m_low, raw))
    held = jnp.where(chip == 0, lead, 0.0) + far[0] + far[1]
    near = spread_near(held)
    part = exchange(raw)
    part, _ = lax.optimization_barrier((part, held))
    gram = exchange(total(column, part, 30))
    near, gram = lax.optimization_barrier((near, gram))
    mine = held + near[0] + near[1]
    other = lax.ppermute(mine, "col", [(i, i ^ 1) for i in range(16)])
    (wide,) = kernel_call(
        wide_kernel, "wide", 6, 1, (column, mine, other, m_high, m_low), (shape(n, blocks * lanes),), (0,) * 5
    )
    gram, wide = lax.optimization_barrier((gram, wide))
    wide = exchange(wide)
    (factor,) = kernel_call(
        factor_kernel, "factor", 12, 1, (column, gram), (shape(3, lanes, lanes),), (0, 0),
        scratch=[pltpu.VMEM((2, lanes, lanes), F32)],
    )
    _, wide = lax.optimization_barrier((factor, wide))
    factor_far = spread_far(factor, chip)
    wide = exchange(total(column, wide))
    near = spread_near(factor_far)
    factor = factor_far + near[0] + near[1]
    half = jax.ShapeDtypeStruct((rows, n), BF16)
    high, low = kernel_call(
        basis_kernel, "basis", 2, 1, (column, mine, other, factor), (half, half), (0, 0, 0, 0, 0)
    )
    chunks = 4
    dma = pltpu.SemaphoreType.DMA
    factors, upper = kernel_call(
        functools.partial(final_kernel, scale, chunks), "finish", 6, 1,
        (column, high, low, m2, wide, factor), (shape(*m2.shape), shape(n * blocks, lanes)), (2,) * 7,
        scratch=[
            pltpu.VMEM((rows, n), BF16), pltpu.VMEM((rows, n), BF16), pltpu.VMEM(m2.shape, F32),
            pltpu.VMEM((n, blocks * lanes), F32), pltpu.VMEM((3, lanes, lanes), F32),
            pltpu.VMEM((n * blocks, lanes), F32), pltpu.VMEM((n, blocks * lanes), BF16),
            pltpu.VMEM((n, blocks * lanes), BF16), dma((4,)), dma((chunks,)), dma((chunks,)), dma(()),
        ],
    )
    return factors.reshape(matrix.shape), upper.reshape(n, blocks, lanes)


def solution(mesh):
    in_specs = (P("row", None, "col"),)
    out_specs = (P("row", None, "col"), P(None, None, "col"))
    return jax.shard_map(shards, mesh=mesh, in_specs=in_specs, out_specs=out_specs, check_vma=False)
```

```python
import functools
import math

import jax
import jax.numpy as jnp
from jax import lax
from jax.experimental import pallas as pl
from jax.experimental.pallas import tpu as pltpu
from jax.sharding import PartitionSpec as P

F32 = jnp.float32
BF16 = jnp.bfloat16
HIGHEST = lax.Precision.HIGHEST
LANES = 128
SUB = 8
RANKS = 16
BUDGET = dict(gram=16, wide=50, turn=24, total=16, factor=16, basis=24, finish=60)


def split(x):
    high = x.astype(BF16)
    low = (x - high.astype(F32)).astype(BF16)
    return high, low


def dot3(a, b):
    left = jnp.concatenate([a[0], a[0], a[1]], axis=1)
    right = jnp.concatenate([b[0], b[1], b[0]], axis=0)
    return jnp.dot(left, right, preferred_element_type=F32)


def dot6(a, b, dims=((1,), (0,))):
    return lax.dot_general(a, b, (dims, ((), ())), precision=HIGHEST, preferred_element_type=F32)


def panels_of(second_core, mine_ref, other_ref):
    mine, other = mine_ref[...], other_ref[...]
    return jnp.concatenate(
        [jnp.where(second_core, other, mine), jnp.where(second_core, mine, other)], axis=1
    )


def gram_kernel(column, mine_ref, other_ref, out_ref):
    panels = panels_of(lax.rem(column[0], 2) == 1, mine_ref, other_ref)
    out_ref[...] = dot6(panels.T, panels)


def turn_kernel(column, mine_ref, out_ref):
    out_ref[0], out_ref[1] = split(mine_ref[...].T)


def wide_kernel(column, mine_ref, other_ref, m_ref, out_ref):
    rows = other_ref.shape[0]
    blocks = m_ref.shape[0] // rows
    swapped = lax.rem(column[0], 2) == 1
    left = [
        jnp.concatenate([jnp.where(swapped, other, mine_ref[i]), jnp.where(swapped, mine_ref[i], other)], axis=0)
        for i, other in enumerate(split(other_ref[...].T))
    ]
    for k in range(0, blocks, 2):
        pair = jnp.concatenate(
            [m_ref[pl.ds(k, rows, stride=blocks), :], m_ref[pl.ds(k + 1, rows, stride=blocks), :]], axis=1
        )
        out_ref[:, k * LANES : (k + 2) * LANES] = dot3(left, split(pair))


def total_kernel(column, part_ref, out_ref):
    piece = part_ref.shape[0] // RANKS
    total = part_ref[0:piece, :]
    for r in range(1, RANKS):
        total = total + part_ref[r * piece : (r + 1) * piece, :]
    for r in range(RANKS):
        out_ref[r * piece : (r + 1) * piece, :] = total


def lower_inverse(tiles):
    count = len(tiles)
    tiles = list(tiles)
    lane = lax.broadcasted_iota(jnp.int32, (SUB, LANES), 1)
    row = lax.broadcasted_iota(jnp.int32, (SUB, LANES), 0)
    whole = lambda x: jnp.broadcast_to(x, (SUB, LANES))
    done = []
    for t in range(count):
        base = SUB * t
        here = tiles[t]
        inside = (lane >= base) & (lane < base + SUB)
        columns = [whole(here[:, base + v : base + v + 1]) for v in range(SUB)]
        d = {(u, v): whole(columns[v][u : u + 1, :]) for u in range(SUB) for v in range(u + 1)}
        l, r = {}, []
        for u in range(SUB):
            r.append(lax.rsqrt(d[u, u]))
            for v in range(u + 1, SUB):
                l[v, u] = d[v, u] * r[u]
            for v in range(u + 1, SUB):
                for w in range(v, SUB):
                    d[w, v] = d[w, v] - l[w, u] * l[v, u]
        start = jnp.where(inside, (lane - base == row).astype(F32), here)
        y = []
        for u in range(SUB):
            total = whole(start[u : u + 1, :])
            for w in range(u):
                total = total - l[u, w] * y[w]
            y.append(total * r[u])
        tile = y[0]
        for u in range(1, SUB):
            tile = jnp.where(row == u, y[u], tile)
        done.append(jnp.where(lane <= row + base, tile, 0.0))
        if t + 1 < count:
            v = [None] * SUB
            for u in reversed(range(SUB)):
                total = y[u]
                for w in range(u + 1, SUB):
                    total = total - l[w, u] * v[w]
                v[u] = total * r[u]
            for i in range(t + 1, count):
                total = jnp.where(inside, 0.0, tiles[i])
                for u in range(SUB):
                    total = total - whole(tiles[i][:, base + u : base + u + 1]) * v[u]
                tiles[i] = total
    return done


def factor_kernel(column, g_ref, x_ref, s_ref):
    n = LANES
    count = n // SUB
    s_ref[0] = g_ref[0:n, 0:n]
    s_ref[1] = g_ref[n : 2 * n, n : 2 * n]

    def turn(step, carry):
        tiles = lower_inverse([s_ref[step, SUB * t : SUB * (t + 1), :] for t in range(count)])
        for t in range(count):
            x_ref[step, SUB * t : SUB * (t + 1), :] = tiles[t]

        @pl.when(step == 0)
        def _():
            r12 = dot6(x_ref[0], g_ref[0:n, n : 2 * n])
            s_ref[1] = s_ref[1] - dot6(r12, r12, ((0,), (0,)))
            s_ref[0] = dot6(r12, x_ref[0], ((0,), (0,)))

        return carry

    lax.fori_loop(0, 2, turn, 0)
    x_ref[2] = -dot6(x_ref[1], s_ref[0])


def whole_inverse(x_ref):
    n = LANES
    return jnp.concatenate(
        [
            jnp.concatenate([x_ref[0], jnp.zeros((n, n), F32)], axis=1),
            jnp.concatenate([x_ref[2], x_ref[1]], axis=1),
        ],
        axis=0,
    )


def basis_kernel(column, mine_ref, other_ref, x_ref, high_ref, low_ref):
    panels = panels_of(lax.rem(column[0], 2) == 1, mine_ref, other_ref)
    high_ref[...], low_ref[...] = split(dot3(split(panels), split(whole_inverse(x_ref).T)))


def final_kernel(
    scale, chunks, column, high_in, low_in, m_in, w_in, x_in, factors_out, upper_out,
    high_ref, low_ref, m_ref, w_ref, x_ref, up_ref, ch_ref, cl_ref, small_sem, in_sem, out_sem, up_sem,
):
    all_rows = high_ref.shape[0]
    rows = all_rows // chunks
    blocks = m_ref.shape[0] // all_rows
    place = column[0]
    n = LANES
    owner = place < 2
    copy = pltpu.make_async_copy
    piece = lambda i: pl.ds(i * rows * blocks, rows * blocks)
    small = [
        copy(src, dst, small_sem.at[i])
        for i, (src, dst) in enumerate(((x_in, x_ref), (w_in, w_ref), (high_in, high_ref), (low_in, low_ref)))
    ]
    for c in small:
        c.start()
    reads = [copy(m_in.at[piece(i), :], m_ref.at[piece(i), :], in_sem.at[i]) for i in range(chunks)]
    writes = [copy(m_ref.at[piece(i), :], factors_out.at[piece(i), :], out_sem.at[i]) for i in range(chunks)]
    for c in reads:
        c.start()
    small[0].wait()
    inverse = split(whole_inverse(x_ref))
    unit = lax.broadcasted_iota(jnp.int32, (2 * n, n), 0) == lax.broadcasted_iota(jnp.int32, (2 * n, n), 1) + place * n
    unit = jnp.where(unit, -scale, 0.0)
    small[1].wait()
    for k in range(0, blocks, 2):
        here = slice(k * n, (k + 2) * n)
        coef = dot3(inverse, split(w_ref[:, here]))
        for j in range(2):
            up_ref[pl.ds(k + j, 2 * n, stride=blocks), :] = coef[:, j * n : (j + 1) * n] * (1.0 / scale)
        if k == 0:
            coef = jnp.concatenate([jnp.where(owner, unit, coef[:, 0:n]), coef[:, n : 2 * n]], axis=1)
        ch_ref[:, here], cl_ref[:, here] = split(coef)
    upper = copy(up_ref, upper_out, up_sem)
    upper.start()
    small[2].wait()
    small[3].wait()
    for i in range(chunks):
        basis = high_ref[i * rows : (i + 1) * rows, :], low_ref[i * rows : (i + 1) * rows, :]
        reads[i].wait()
        for k in range(0, blocks, 2):
            here = slice(k * n, (k + 2) * n)
            change = dot3(basis, (ch_ref[:, here], cl_ref[:, here]))
            for j in range(2):
                at = pl.ds(i * rows * blocks + k + j, rows, stride=blocks)
                old = m_ref[at, :]
                if k + j == 0:
                    old = jnp.where(owner, 0.0, old)
                m_ref[at, :] = old - change[:, j * n : (j + 1) * n]
        writes[i].start()
    upper.wait()
    for c in writes:
        c.wait()


IN_SMEM = pl.BlockSpec(memory_space=pltpu.SMEM)
ANYWHERE = pl.BlockSpec(memory_space=pl.ANY)


def by_rows(array, steps):
    return pl.BlockSpec((array.shape[0] // steps, array.shape[1]), lambda i: (i, 0))


def by_columns(array, steps):
    return pl.BlockSpec((array.shape[0], array.shape[1] // steps), lambda i: (0, i))


def fixed(array):
    return pl.BlockSpec(array.shape, lambda i: (0,) * len(array.shape))


def kernel_call(body, name, micros, steps, operands, out_shape, row_split, scratch=()):
    specs = [by_rows(x, steps) if s == 1 else ANYWHERE if s == 2 else by_columns(x, steps) if s == 3 else fixed(x) for x, s in zip((*operands[1:], *out_shape), row_split)]
    return pl.pallas_call(
        body,
        grid=(steps,),
        out_shape=out_shape,
        in_specs=[IN_SMEM] + specs[: len(operands) - 1],
        out_specs=tuple(specs[len(operands) - 1 :]),
        scratch_shapes=list(scratch),
        compiler_params=pltpu.CompilerParams(vmem_limit_bytes=BUDGET[name] * 2**20),
        cost_estimate=pl.CostEstimate(flops=micros * 10**9, bytes_accessed=micros * 10**6, transcendentals=0),
        name=name,
    )(*operands)


def shape(*dims):
    return jax.ShapeDtypeStruct(dims, F32)


def both_cores(pairs):
    return [(2 * a + c, 2 * b + c) for a, b in pairs for c in range(2)]


def by_core(first, second):
    return [(2 * a, 2 * b) for a, b in first] + [(2 * a + 1, 2 * b + 1) for a, b in second]


def send(x, pairs):
    return lax.ppermute(x, "col", both_cores(pairs))


def spread_far(x, chip):
    far = send(x, [(0, 3)]), send(x, [(0, 5)])
    return jnp.where(chip == 0, x, 0.0) + far[0] + far[1]


def spread_near(x):
    return send(x, [(0, 1), (3, 4), (5, 6)]), send(x, [(0, 7), (3, 2)])


def total(column, part, micros=1):
    return kernel_call(total_kernel, "total", micros, 1, (column, part), (shape(*part.shape),), (0, 0))[0]


def exchange(x):
    return lax.all_to_all(x, "row", 0, 0, tiled=True)


def shards(matrix):
    rows, blocks, lanes = matrix.shape
    size = lax.axis_size("row")
    scale = math.sqrt(rows * size)
    steps = 4
    m2 = matrix.reshape(rows * blocks, lanes)
    column = lax.axis_index("col").astype(jnp.int32).reshape(1)
    chip = lax.axis_index("col") // 2
    lead = matrix[:, 0, :]
    n = 2 * lanes
    partner = lax.ppermute(lead, "col", [(0, 1), (1, 0)])
    (part,) = kernel_call(gram_kernel, "gram", 3, 1, (column, lead, partner), (shape(n, n),), (0, 0, 0))
    lead, part = lax.optimization_barrier((lead, part))
    hop = lambda x, first, second: lax.ppermute(x, "col", by_core(first, second))
    part = exchange(part)
    first = hop(lead, [(0, 3)], [(0, 5)])
    held = jnp.where(chip == 0, lead, 0.0) + first
    part, _ = lax.optimization_barrier((part, held))
    near = hop(held, [(0, 7), (3, 4)], [(0, 1), (5, 6)]), hop(held, [(3, 2)], [(5, 4)])
    summed = total(column, part, 30)
    near, summed = lax.optimization_barrier((near, summed))
    more = held + near[0] + near[1]
    gram = exchange(summed)
    last = hop(more, [(2, 1), (4, 5), (7, 6)], [(6, 7), (4, 3), (1, 2)])
    mine = more + last
    other = lax.ppermute(mine, "col", [(i, i ^ 1) for i in range(16)])
    (turned,) = kernel_call(
        turn_kernel, "turn", 40, 1, (column, mine), (jax.ShapeDtypeStruct((2, lanes, rows), BF16),), (0, 0)
    )
    (wide,) = kernel_call(
        wide_kernel, "wide", 6, 1, (column, turned, other, m2), (shape(n, blocks * lanes),), (0,) * 4
    )
    gram, wide = lax.optimization_barrier((gram, wide))
    wide = exchange(wide)
    (factor,) = kernel_call(
        factor_kernel, "factor", 12, 1, (column, gram), (shape(3, lanes, lanes),), (0, 0),
        scratch=[pltpu.VMEM((2, lanes, lanes), F32)],
    )
    _, wide = lax.optimization_barrier((factor, wide))
    factor_far = spread_far(factor, chip)
    wide = exchange(total(column, wide))
    near = spread_near(factor_far)
    factor = factor_far + near[0] + near[1]
    half = jax.ShapeDtypeStruct((rows, n), BF16)
    high, low = kernel_call(
        basis_kernel, "basis", 2, 1, (column, mine, other, factor), (half, half), (0, 0, 0, 0, 0)
    )
    chunks = 4
    dma = pltpu.SemaphoreType.DMA
    factors, upper = kernel_call(
        functools.partial(final_kernel, scale, chunks), "finish", 6, 1,
        (column, high, low, m2, wide, factor), (shape(*m2.shape), shape(n * blocks, lanes)), (2,) * 7,
        scratch=[
            pltpu.VMEM((rows, n), BF16), pltpu.VMEM((rows, n), BF16), pltpu.VMEM(m2.shape, F32),
            pltpu.VMEM((n, blocks * lanes), F32), pltpu.VMEM((3, lanes, lanes), F32),
            pltpu.VMEM((n * blocks, lanes), F32), pltpu.VMEM((n, blocks * lanes), BF16),
            pltpu.VMEM((n, blocks * lanes), BF16), dma((4,)), dma((chunks,)), dma((chunks,)), dma(()),
        ],
    )
    return factors.reshape(matrix.shape), upper.reshape(n, blocks, lanes)


def solution(mesh):
    in_specs = (P("row", None, "col"),)
    out_specs = (P("row", None, "col"), P(None, None, "col"))
    return jax.shard_map(shards, mesh=mesh, in_specs=in_specs, out_specs=out_specs, check_vma=False)
```

```python
import functools
import math

import jax
import jax.numpy as jnp
from jax import lax
from jax.experimental import pallas as pl
from jax.experimental.pallas import tpu as pltpu
from jax.sharding import PartitionSpec as P

F32 = jnp.float32
BF16 = jnp.bfloat16
HIGHEST = lax.Precision.HIGHEST
LANES = 128
SUB = 8
RANKS = 16
BUDGET = dict(gram=16, halves=60, wide=32, total=16, factor=16, basis=24, finish=60)


def split(x):
    high = x.astype(BF16)
    low = (x - high.astype(F32)).astype(BF16)
    return high, low


def dot3(a, b):
    left = jnp.concatenate([a[0], a[0], a[1]], axis=1)
    right = jnp.concatenate([b[0], b[1], b[0]], axis=0)
    return jnp.dot(left, right, preferred_element_type=F32)


def dot6(a, b, dims=((1,), (0,))):
    return lax.dot_general(a, b, (dims, ((), ())), precision=HIGHEST, preferred_element_type=F32)


def panels_of(second_core, mine_ref, other_ref):
    mine, other = mine_ref[...], other_ref[...]
    return jnp.concatenate(
        [jnp.where(second_core, other, mine), jnp.where(second_core, mine, other)], axis=1
    )


def gram_kernel(column, mine_ref, other_ref, out_ref):
    panels = panels_of(lax.rem(column[0], 2) == 1, mine_ref, other_ref)
    out_ref[...] = dot6(panels.T, panels)


def halves_kernel(column, m_ref, high_ref, low_ref):
    blocks = m_ref.shape[0] // high_ref.shape[0]
    for k in range(blocks):
        here = slice(k * LANES, (k + 1) * LANES)
        high_ref[:, here], low_ref[:, here] = split(m_ref[pl.ds(k, high_ref.shape[0], stride=blocks), :])


def wide_kernel(column, mine_ref, other_ref, high_ref, low_ref, out_ref):
    left = split(panels_of(lax.rem(column[0], 2) == 1, mine_ref, other_ref).T)
    step = 2 * LANES
    for k in range(0, out_ref.shape[1], step):
        here = slice(k, k + step)
        out_ref[:, here] = dot3(left, (high_ref[:, here], low_ref[:, here]))


def total_kernel(column, part_ref, out_ref):
    piece = part_ref.shape[0] // RANKS
    total = part_ref[0:piece, :]
    for r in range(1, RANKS):
        total = total + part_ref[r * piece : (r + 1) * piece, :]
    for r in range(RANKS):
        out_ref[r * piece : (r + 1) * piece, :] = total


def lower_inverse(tiles):
    count = len(tiles)
    tiles = list(tiles)
    lane = lax.broadcasted_iota(jnp.int32, (SUB, LANES), 1)
    row = lax.broadcasted_iota(jnp.int32, (SUB, LANES), 0)
    whole = lambda x: jnp.broadcast_to(x, (SUB, LANES))
    done = []
    for t in range(count):
        base = SUB * t
        here = tiles[t]
        inside = (lane >= base) & (lane < base + SUB)
        columns = [whole(here[:, base + v : base + v + 1]) for v in range(SUB)]
        d = {(u, v): whole(columns[v][u : u + 1, :]) for u in range(SUB) for v in range(u + 1)}
        l, r = {}, []
        for u in range(SUB):
            r.append(lax.rsqrt(d[u, u]))
            for v in range(u + 1, SUB):
                l[v, u] = d[v, u] * r[u]
            for v in range(u + 1, SUB):
                for w in range(v, SUB):
                    d[w, v] = d[w, v] - l[w, u] * l[v, u]
        start = jnp.where(inside, (lane - base == row).astype(F32), here)
        y = []
        for u in range(SUB):
            total = whole(start[u : u + 1, :])
            for w in range(u):
                total = total - l[u, w] * y[w]
            y.append(total * r[u])
        tile = y[0]
        for u in range(1, SUB):
            tile = jnp.where(row == u, y[u], tile)
        done.append(jnp.where(lane <= row + base, tile, 0.0))
        if t + 1 < count:
            v = [None] * SUB
            for u in reversed(range(SUB)):
                total = y[u]
                for w in range(u + 1, SUB):
                    total = total - l[w, u] * v[w]
                v[u] = total * r[u]
            for i in range(t + 1, count):
                total = jnp.where(inside, 0.0, tiles[i])
                for u in range(SUB):
                    total = total - whole(tiles[i][:, base + u : base + u + 1]) * v[u]
                tiles[i] = total
    return done


def factor_kernel(column, g_ref, x_ref, s_ref):
    n = LANES
    count = n // SUB
    s_ref[0] = g_ref[0:n, 0:n]
    s_ref[1] = g_ref[n : 2 * n, n : 2 * n]

    def turn(step, carry):
        tiles = lower_inverse([s_ref[step, SUB * t : SUB * (t + 1), :] for t in range(count)])
        for t in range(count):
            x_ref[step, SUB * t : SUB * (t + 1), :] = tiles[t]

        @pl.when(step == 0)
        def _():
            r12 = dot6(x_ref[0], g_ref[0:n, n : 2 * n])
            s_ref[1] = s_ref[1] - dot6(r12, r12, ((0,), (0,)))
            s_ref[0] = dot6(r12, x_ref[0], ((0,), (0,)))

        return carry

    lax.fori_loop(0, 2, turn, 0)
    x_ref[2] = -dot6(x_ref[1], s_ref[0])


def whole_inverse(x_ref):
    n = LANES
    return jnp.concatenate(
        [
            jnp.concatenate([x_ref[0], jnp.zeros((n, n), F32)], axis=1),
            jnp.concatenate([x_ref[2], x_ref[1]], axis=1),
        ],
        axis=0,
    )


def basis_kernel(column, mine_ref, other_ref, x_ref, high_ref, low_ref):
    panels = panels_of(lax.rem(column[0], 2) == 1, mine_ref, other_ref)
    high_ref[...], low_ref[...] = split(dot3(split(panels), split(whole_inverse(x_ref).T)))


def final_kernel(
    scale, chunks, column, high_in, low_in, m_in, w_in, x_in, factors_out, upper_out,
    high_ref, low_ref, m_ref, w_ref, x_ref, up_ref, ch_ref, cl_ref, small_sem, in_sem, out_sem, up_sem,
):
    all_rows = high_ref.shape[0]
    rows = all_rows // chunks
    blocks = m_ref.shape[0] // all_rows
    place = column[0]
    n = LANES
    owner = place < 2
    copy = pltpu.make_async_copy
    piece = lambda i: pl.ds(i * rows * blocks, rows * blocks)
    small = [
        copy(src, dst, small_sem.at[i])
        for i, (src, dst) in enumerate(((x_in, x_ref), (w_in, w_ref), (high_in, high_ref), (low_in, low_ref)))
    ]
    for c in small:
        c.start()
    reads = [copy(m_in.at[piece(i), :], m_ref.at[piece(i), :], in_sem.at[i]) for i in range(chunks)]
    writes = [copy(m_ref.at[piece(i), :], factors_out.at[piece(i), :], out_sem.at[i]) for i in range(chunks)]
    for c in reads:
        c.start()
    small[0].wait()
    inverse = split(whole_inverse(x_ref))
    unit = lax.broadcasted_iota(jnp.int32, (2 * n, n), 0) == lax.broadcasted_iota(jnp.int32, (2 * n, n), 1) + place * n
    unit = jnp.where(unit, -scale, 0.0)
    small[1].wait()
    for k in range(0, blocks, 2):
        here = slice(k * n, (k + 2) * n)
        coef = dot3(inverse, split(w_ref[:, here]))
        for j in range(2):
            up_ref[pl.ds(k + j, 2 * n, stride=blocks), :] = coef[:, j * n : (j + 1) * n] * (1.0 / scale)
        if k == 0:
            coef = jnp.concatenate([jnp.where(owner, unit, coef[:, 0:n]), coef[:, n : 2 * n]], axis=1)
        ch_ref[:, here], cl_ref[:, here] = split(coef)
    upper = copy(up_ref, upper_out, up_sem)
    upper.start()
    small[2].wait()
    small[3].wait()
    for i in range(chunks):
        basis = high_ref[i * rows : (i + 1) * rows, :], low_ref[i * rows : (i + 1) * rows, :]
        reads[i].wait()
        for k in range(0, blocks, 2):
            here = slice(k * n, (k + 2) * n)
            change = dot3(basis, (ch_ref[:, here], cl_ref[:, here]))
            for j in range(2):
                at = pl.ds(i * rows * blocks + k + j, rows, stride=blocks)
                old = m_ref[at, :]
                if k + j == 0:
                    old = jnp.where(owner, 0.0, old)
                m_ref[at, :] = old - change[:, j * n : (j + 1) * n]
        writes[i].start()
    upper.wait()
    for c in writes:
        c.wait()


IN_SMEM = pl.BlockSpec(memory_space=pltpu.SMEM)
ANYWHERE = pl.BlockSpec(memory_space=pl.ANY)


def by_rows(array, steps):
    return pl.BlockSpec((array.shape[0] // steps, array.shape[1]), lambda i: (i, 0))


def fixed(array):
    return pl.BlockSpec(array.shape, lambda i: (0,) * len(array.shape))


def kernel_call(body, name, micros, steps, operands, out_shape, row_split, scratch=()):
    specs = [by_rows(x, steps) if s == 1 else ANYWHERE if s == 2 else fixed(x) for x, s in zip((*operands[1:], *out_shape), row_split)]
    return pl.pallas_call(
        body,
        grid=(steps,),
        out_shape=out_shape,
        in_specs=[IN_SMEM] + specs[: len(operands) - 1],
        out_specs=tuple(specs[len(operands) - 1 :]),
        scratch_shapes=list(scratch),
        compiler_params=pltpu.CompilerParams(vmem_limit_bytes=BUDGET[name] * 2**20),
        cost_estimate=pl.CostEstimate(flops=micros * 10**9, bytes_accessed=micros * 10**6, transcendentals=0),
        name=name,
    )(*operands)


def shape(*dims):
    return jax.ShapeDtypeStruct(dims, F32)


def both_cores(pairs):
    return [(2 * a + c, 2 * b + c) for a, b in pairs for c in range(2)]


def send(x, pairs):
    return lax.ppermute(x, "col", both_cores(pairs))


def spread_far(x, chip):
    far = send(x, [(0, 3)]), send(x, [(0, 5)])
    return jnp.where(chip == 0, x, 0.0) + far[0] + far[1]


def spread_near(x):
    return send(x, [(0, 1), (3, 4), (5, 6)]), send(x, [(0, 7), (3, 2)])


def total(column, part, micros=1):
    return kernel_call(total_kernel, "total", micros, 1, (column, part), (shape(*part.shape),), (0, 0))[0]


def exchange(x):
    return lax.all_to_all(x, "row", 0, 0, tiled=True)


def shards(matrix):
    rows, blocks, lanes = matrix.shape
    size = lax.axis_size("row")
    scale = math.sqrt(rows * size)
    steps = 4
    m2 = matrix.reshape(rows * blocks, lanes)
    column = lax.axis_index("col").astype(jnp.int32).reshape(1)
    chip = lax.axis_index("col") // 2
    lead = matrix[:, 0, :]
    n = 2 * lanes
    partner = lax.ppermute(lead, "col", [(0, 1), (1, 0)])
    (part,) = kernel_call(gram_kernel, "gram", 3, 1, (column, lead, partner), (shape(n, n),), (0, 0, 0))
    half = jax.ShapeDtypeStruct((rows, blocks * lanes), BF16)
    later, raw = lax.optimization_barrier((column, part))
    m_high, m_low = kernel_call(halves_kernel, "halves", 4, steps, (later, m2), (half, half), (1, 1, 1))
    lead, raw = lax.optimization_barrier((lead, raw))
    far = send(lead, [(0, 3)]), send(lead, [(0, 5)])
    far, _, _, _ = lax.optimization_barrier((far, m_high, m_low, raw))
    held = jnp.where(chip == 0, lead, 0.0) + far[0] + far[1]
    near = spread_near(held)
    part = exchange(raw)
    part, _ = lax.optimization_barrier((part, held))
    gram = exchange(total(column, part, 30))
    near, gram = lax.optimization_barrier((near, gram))
    mine = held + near[0] + near[1]
    other = lax.ppermute(mine, "col", [(i, i ^ 1) for i in range(16)])
    (wide,) = kernel_call(
        wide_kernel, "wide", 6, 1, (column, mine, other, m_high, m_low), (shape(n, blocks * lanes),), (0,) * 5
    )
    gram, wide = lax.optimization_barrier((gram, wide))
    wide = exchange(wide)
    (factor,) = kernel_call(
        factor_kernel, "factor", 12, 1, (column, gram), (shape(3, lanes, lanes),), (0, 0),
        scratch=[pltpu.VMEM((2, lanes, lanes), F32)],
    )
    _, wide = lax.optimization_barrier((factor, wide))
    factor_far = spread_far(factor, chip)
    wide = exchange(total(column, wide))
    near = spread_near(factor_far)
    factor = factor_far + near[0] + near[1]
    half = jax.ShapeDtypeStruct((rows, n), BF16)
    high, low = kernel_call(
        basis_kernel, "basis", 2, 1, (column, mine, other, factor), (half, half), (0, 0, 0, 0, 0)
    )
    chunks = 4
    dma = pltpu.SemaphoreType.DMA
    factors, upper = kernel_call(
        functools.partial(final_kernel, scale, chunks), "finish", 6, 1,
        (column, high, low, m2, wide, factor), (shape(*m2.shape), shape(n * blocks, lanes)), (2,) * 7,
        scratch=[
            pltpu.VMEM((rows, n), BF16), pltpu.VMEM((rows, n), BF16), pltpu.VMEM(m2.shape, F32),
            pltpu.VMEM((n, blocks * lanes), F32), pltpu.VMEM((3, lanes, lanes), F32),
            pltpu.VMEM((n * blocks, lanes), F32), pltpu.VMEM((n, blocks * lanes), BF16),
            pltpu.VMEM((n, blocks * lanes), BF16), dma((4,)), dma((chunks,)), dma((chunks,)), dma(()),
        ],
    )
    return factors.reshape(matrix.shape), upper.reshape(n, blocks, lanes)


def solution(mesh):
    in_specs = (P("row", None, "col"),)
    out_specs = (P("row", None, "col"), P(None, None, "col"))
    return jax.shard_map(shards, mesh=mesh, in_specs=in_specs, out_specs=out_specs, check_vma=False)
```
